32 devices in a mesh: kc: 8 (over z, core), ia: 4 (over y, x).
Axes of the slice: x: 2, y: 2, z: 4, core: 2. Of those that a mesh axis runs over, the one named last changes fastest.
Arguments:
- amplitudes: bfloat16 [32768, 32768], P('ia', 'kc'), may hold values from -0.03125 to 0.03125
- occupied_factors: bfloat16 [2048, 4096], P('kc'), may hold values from -0.1875 to 0.1875
- virtual_factors: bfloat16 [2048, 4096], P('kc', 'ia'), may hold values from -6 to 6
Outputs:
- residual: float32 [32768, 512], P('ia', 'kc')
The draws below stay inside these ranges and needn't reach their ends.
All inputs are finite; a program needn't handle non-finite values.
Results may differ from the reference program's by a relative error of at most 0.0029.
Values may be sent and summed in bfloat16 or wider, within the bound.
A program may use at most 128 MiB of HBM per device.

```python
import jax
import jax.numpy as jnp
from jax import lax

O = 64
V = 512
Q = 2048
BW = 8


def spiked(array, stream_key, source, target, shards_of, factor):
    owner, partner = [(jnp.arange(array.shape[position]) // (array.shape[position] // shards_of)).reshape([-1 if axis == position else 1 for axis in range(array.ndim)]) for position in (source, target)]
    chosen = jax.random.permutation(stream_key, shards_of)[partner]
    strong = (owner == chosen) | (owner == (partner + shards_of // 2) % shards_of)
    return jnp.where(strong, factor * array, array)


def shard_levels(rng, dims, cuts, least, high):
    def one(axis_at, shards_of):
        steps = jax.random.uniform(jax.random.fold_in(jax.random.fold_in(rng, 6), axis_at), (shards_of,), jnp.float32, least / len(cuts), high / len(cuts))
        return jnp.repeat(jnp.exp(steps), dims[axis_at] // shards_of).reshape((-1,) + (1,) * (len(dims) - axis_at - 1))

    gain = one(*cuts[0])
    for cut in cuts[1:]:
        gain = gain * one(*cut)
    return gain


def gaussian(own_key, dims, deviation, most, split=(), held_as=jnp.bfloat16):
    values = jax.random.normal(own_key, dims, jnp.float32) * deviation
    if len(split) > 0:
        values = shard_levels(own_key, dims, split, -0.22, 0.18) * values
    return jnp.clip(values, min=-most, max=most).astype(held_as)


def heavy_noise(own_key, extent, width, bound, pieces, heavy, held_as=jnp.bfloat16):
    entries = width * jax.random.normal(own_key, extent, jnp.float32)
    if pieces:
        entries = entries * shard_levels(own_key, extent, pieces, -0.22, 0.18)
    return jnp.clip(spiked(entries, jax.random.fold_in(own_key, 3), *heavy), -bound, bound).astype(held_as)


def setup_inputs(seed: int = 0) -> dict:
    splits = jax.random.split(jax.random.key(seed), 4)
    return {
        "amplitudes": gaussian(splits[0], (O * V, O * V), (O * V) ** -0.5, 0.03125, ((0, 4), (1, 8))),
        "occupied_factors": heavy_noise(splits[1], (Q, O * O), Q ** -0.5, 0.1875, ((0, 8),), (0, 1, 8, 2.0)),
        "virtual_factors": gaussian(splits[2], (Q, V * BW), 1.0, 6.0, ((0, 8), (1, 4))),
    }


def reference(amplitudes, occupied_factors, virtual_factors):
    integrals = jnp.dot(occupied_factors.T, virtual_factors, preferred_element_type=jnp.float32).astype(jnp.bfloat16)
    cycle_block = integrals.reshape(O, O, V, BW).transpose(0, 2, 1, 3).reshape(O * V, O * BW)

    def one_block(amplitude_rows):
        return jnp.dot(amplitude_rows, cycle_block, preferred_element_type=jnp.float32)

    blocks = lax.map(one_block, amplitudes.reshape(O, V, O * V))
    return blocks.reshape(O * V, O * BW)
```

```python
import functools

import jax
import jax.numpy as jnp
from jax import lax
from jax.experimental import pallas as pl
from jax.experimental.pallas import tpu as pltpu
from jax.sharding import PartitionSpec as P

O = 64
V = 512
BW = 8
MESH = pl.DeviceIdType.MESH


def reduce_kernel(
    n, count, rows, a_ref, b_ref, o_ref,
    abuf, pair_out, pair_in, total, onward, from_left, from_right, kept, given,
    a_sem, pair_s, pair_r, right_s, right_r, left_s, left_r, kept_sem, given_s, given_r,
):
    me = lax.axis_index("kc")
    z, core = me // 2, me % 2
    width = b_ref.shape[1] // n
    half = width // 2
    partner = z * 2 + (1 - core)
    right, left = me + 2, me - 2

    def fetch(t, own):
        chunk = 2 * t + (core if own else 1 - core)
        start = pl.multiple_of(chunk * rows, rows)
        slot = 1 if own else 0
        return pltpu.make_async_copy(a_ref.at[pl.ds(start, rows)], abuf.at[slot], a_sem.at[slot])

    def pair(t):
        return pltpu.make_async_remote_copy(
            src_ref=pair_out.at[t], dst_ref=pair_in.at[t], send_sem=pair_s.at[t],
            recv_sem=pair_r.at[t], device_id={"kc": partner}, device_id_type=MESH)

    def go_right(t, d):
        return pltpu.make_async_remote_copy(
            src_ref=onward.at[t, d], dst_ref=from_left.at[t, d], send_sem=right_s.at[t, d],
            recv_sem=right_r.at[t, d], device_id={"kc": right}, device_id_type=MESH)

    def go_left(t, d):
        return pltpu.make_async_remote_copy(
            src_ref=onward.at[t, d], dst_ref=from_right.at[t, d], send_sem=left_s.at[t, d],
            recv_sem=left_r.at[t, d], device_id={"kc": left}, device_id_type=MESH)

    def keep(t):
        start = pl.multiple_of((2 * t + core) * rows, rows)
        return pltpu.make_async_copy(kept.at[t], o_ref.at[pl.ds(start, rows)], kept_sem.at[t])

    def give(t, whose):
        start = pl.multiple_of((2 * t + whose) * rows, rows)
        return pltpu.make_async_remote_copy(
            src_ref=given.at[t], dst_ref=o_ref.at[pl.ds(start, rows)], send_sem=given_s.at[t],
            recv_sem=given_r.at[t], device_id={"kc": partner}, device_id_type=MESH)

    fetch(0, False).start()
    barrier = pltpu.get_barrier_semaphore()
    pl.semaphore_signal(barrier, inc=1, device_id={"kc": partner}, device_id_type=MESH)

    @pl.when(z > 0)
    def _():
        pl.semaphore_signal(barrier, inc=1, device_id={"kc": left}, device_id_type=MESH)

    @pl.when(z < n - 1)
    def _():
        pl.semaphore_signal(barrier, inc=1, device_id={"kc": right}, device_id_type=MESH)

    pl.semaphore_wait(barrier, 1 + jnp.where(z > 0, 1, 0) + jnp.where(z < n - 1, 1, 0))

    def columns(t, d):
        return total[t, :, d * width:(d + 1) * width]

    def step(t, carry):
        @pl.when(t < count)
        def _():
            fetch(t, False).wait()
            fetch(t, True).start()
            product = jnp.dot(abuf[0], b_ref[...], preferred_element_type=jnp.float32)
            pair_out[t] = product.astype(jnp.bfloat16)
            pair(t).start()
            fetch(t, True).wait()

            @pl.when(t + 1 < count)
            def _():
                fetch(t + 1, False).start()

            total[t] = jnp.dot(abuf[1], b_ref[...], preferred_element_type=jnp.float32)
            pair(t).wait_recv()
            total[t] += pair_in[t].astype(jnp.float32)

        tr = t - z

        @pl.when((tr >= 0) & (tr < count))
        def _():
            for d in reversed(range(1, n)):
                @pl.when((d > z) & (z == 0))
                def _():
                    onward[tr, d] = columns(tr, d).astype(jnp.bfloat16)
                    go_right(tr, d).start()

                @pl.when((d > z) & (z > 0))
                def _():
                    go_right(tr, d).wait_recv()
                    onward[tr, d] = (columns(tr, d) + from_left[tr, d].astype(jnp.float32)).astype(jnp.bfloat16)
                    go_right(tr, d).start()

        tl = t - (n - 1 - z)

        @pl.when((tl >= 0) & (tl < count))
        def _():
            for d in range(n - 1):
                @pl.when((d < z) & (z == n - 1))
                def _():
                    onward[tl, d] = columns(tl, d).astype(jnp.bfloat16)
                    go_left(tl, d).start()

                @pl.when((d < z) & (z < n - 1))
                def _():
                    go_left(tl, d).wait_recv()
                    onward[tl, d] = (columns(tl, d) + from_right[tl, d].astype(jnp.float32)).astype(jnp.bfloat16)
                    go_left(tl, d).start()

        tf = t - jnp.maximum(z, n - 1 - z)

        @pl.when((tf >= 0) & (tf < count))
        def _():
            for d in range(n):
                @pl.when(d == z)
                def _():
                    value = columns(tf, d)
                    if d > 0:
                        go_right(tf, d).wait_recv()
                        value += from_left[tf, d].astype(jnp.float32)
                    if d < n - 1:
                        go_left(tf, d).wait_recv()
                        value += from_right[tf, d].astype(jnp.float32)

                    @pl.when(core == 0)
                    def _():
                        kept[tf] = value[:, :half]
                        given[tf] = value[:, half:]

                    @pl.when(core == 1)
                    def _():
                        kept[tf] = value[:, half:]
                        given[tf] = value[:, :half]

            keep(tf).start()
            give(tf, core).start()

        return carry

    lax.fori_loop(0, count + n - 1, step, 0)

    def drain(t, carry):
        pair(t).wait_send()
        keep(t).wait()
        give(t, core).wait_send()
        give(t, 1 - core).wait_recv()
        for d in range(n):
            @pl.when(d > z)
            def _():
                go_right(t, d).wait_send()

            @pl.when(d < z)
            def _():
                go_left(t, d).wait_send()
        return carry

    lax.fori_loop(0, count, drain, 0)


def gemm_reduce_scatter(amplitudes, cycle_block, devices):
    local_rows, depth = amplitudes.shape
    columns = cycle_block.shape[1]
    n = devices // 2
    rows = min(512, local_rows // 2)
    count = local_rows // (2 * rows)
    width = columns // n
    bf, f32 = jnp.bfloat16, jnp.float32
    dma = pltpu.SemaphoreType.DMA
    return pl.pallas_call(
        functools.partial(reduce_kernel, n, count, rows),
        out_shape=jax.ShapeDtypeStruct((local_rows, width // 2), f32),
        in_specs=[pl.BlockSpec(memory_space=pl.ANY), pl.BlockSpec(memory_space=pltpu.VMEM)],
        out_specs=pl.BlockSpec(memory_space=pl.ANY),
        scratch_shapes=[
            pltpu.VMEM((2, rows, depth), bf),
            pltpu.VMEM((count, rows, columns), bf),
            pltpu.VMEM((count, rows, columns), bf),
            pltpu.VMEM((count, rows, columns), f32),
            pltpu.VMEM((count, n, rows, width), bf),
            pltpu.VMEM((count, n, rows, width), bf),
            pltpu.VMEM((count, n, rows, width), bf),
            pltpu.VMEM((count, rows, width // 2), f32),
            pltpu.VMEM((count, rows, width // 2), f32),
            dma((2,)), dma((count,)), dma((count,)),
            dma((count, n)), dma((count, n)), dma((count, n)), dma((count, n)),
            dma((count,)), dma((count,)), dma((count,)),
        ],
        compiler_params=pltpu.CompilerParams(
            collective_id=0, has_side_effects=True, vmem_limit_bytes=60 * 2**20),
    )(amplitudes, cycle_block)


def per_device(amplitudes, occupied_factors, virtual_factors):
    aux_local = occupied_factors.shape[0]
    k_per_device = O // lax.axis_size("kc")
    c_per_device = V // lax.axis_size("ia")
    shaped = occupied_factors.reshape(aux_local, O, O)
    regrouped = lax.all_to_all(shaped, "kc", split_axis=1, concat_axis=0, tiled=True)
    virtual_all = lax.all_gather(virtual_factors, "kc", axis=0, tiled=True)
    summed = lax.dot_general(
        regrouped.reshape(-1, k_per_device * O),
        virtual_all,
        (((0,), (0,)), ((), ())),
        preferred_element_type=jnp.float32,
    )
    integrals = summed.astype(jnp.bfloat16)
    blocks = (
        integrals.reshape(k_per_device, O, c_per_device, BW)
        .transpose(0, 2, 1, 3)
        .reshape(k_per_device, c_per_device, O * BW)
    )
    gathered = lax.all_gather(blocks, "ia", axis=1, tiled=True)
    cycle_block = gathered.reshape(k_per_device * V, O * BW)
    return gemm_reduce_scatter(amplitudes, cycle_block, lax.axis_size("kc"))


def solution(mesh):
    placed = (P("ia", "kc"), P("kc", None), P("kc", "ia"))
    return jax.shard_map(
        per_device, mesh=mesh, in_specs=placed, out_specs=P("ia", "kc"), check_vma=False
    )
```

```python
import functools

import jax
import jax.numpy as jnp
from jax import lax
from jax.experimental import pallas as pl
from jax.experimental.pallas import tpu as pltpu
from jax.sharding import PartitionSpec as P

O = 64
V = 512
BW = 8
MESH = pl.DeviceIdType.MESH


class Spread:
    def __init__(self, view, own, kind, groups, send, recv):
        self.view, self.own, self.kind, self.send, self.recv = view, own, kind, send, recv
        self.a = 2
        self.b = groups // 2
        me = lax.axis_index("ia")
        self.p, self.q = me // self.b, me % self.b

    def at(self, r, s):
        return lax.rem(self.p + s + self.a, self.a) * self.b + lax.rem(self.q + r + self.b, self.b)

    def copy(self, source, r, s, target):
        return pltpu.make_async_remote_copy(
            src_ref=self.view(self.at(*source)) if source != (0, 0) else self.own,
            dst_ref=self.view(self.at(*source)), send_sem=self.send.at[r, s],
            recv_sem=self.recv.at[r, s], device_id={"ia": self.at(*target)}, device_id_type=MESH)

    def sends(self, direct):
        out = []
        for r in range(self.b):
            for s in range(self.a):
                if r and s and not direct:
                    out.append(self.copy((-r, 0), r, s, (0, s)) if self.kind == 0
                               else self.copy((0, -s), r, s, (r, 0)))
                elif (r or s) and not (r and s) and direct:
                    out.append(self.copy((0, 0), r, s, (r, s)))
        return out

    def arrived(self, r, s):
        pltpu.make_async_remote_copy(
            src_ref=self.view(self.at(-r, -s)), dst_ref=self.view(self.at(-r, -s)),
            send_sem=self.send.at[r, s], recv_sem=self.recv.at[r, s],
            device_id={"ia": self.at(r, s)}, device_id_type=MESH).wait_recv()

    def start(self):
        order = self.sends(True)
        for copy in order if self.kind else reversed(order):
            copy.start()

    def relay(self):
        if self.kind == 0:
            for r in range(1, self.b):
                self.arrived(r, 0)
        else:
            for s in range(1, self.a):
                self.arrived(0, s)
        for copy in self.sends(False):
            copy.start()

    def finish(self):
        for r in range(self.b):
            for s in range(self.a):
                first = (s == 0) if self.kind == 0 else (r == 0)
                if (r or s) and not first:
                    self.arrived(r, s)

    def drain(self):
        for copy in self.sends(True) + self.sends(False):
            copy.wait_send()


def signal_all(barrier, axis, size):
    me = lax.axis_index(axis)
    for step in range(1, size):
        pl.semaphore_signal(barrier, inc=1, device_id={axis: lax.rem(me + step, size)}, device_id_type=MESH)


def factors_kernel(
    devices, groups, occ_ref, virt_ref, out_ref, occ, virt,
    o_s, o_r, g_s, g_r, right_s, left_s, v_r, pair_s, pair_r,
):
    n = devices // 2
    me, ia = lax.axis_index("kc"), lax.axis_index("ia")
    z, core = me // 2, me % 2
    share = occ_ref.shape[0] // groups
    cols = occ_ref.shape[1] // devices

    barrier = pltpu.get_barrier_semaphore()
    signal_all(barrier, "kc", devices)
    signal_all(barrier, "ia", groups)
    pl.semaphore_wait(barrier, devices + groups - 2)

    def direct(step):
        to = lax.rem(me + step, devices)
        return pltpu.make_async_remote_copy(
            src_ref=occ_ref.at[pl.ds(pl.multiple_of(ia * share, share), share),
                               pl.ds(pl.multiple_of(to * cols, cols), cols)],
            dst_ref=occ.at[me, ia], send_sem=o_s.at[step], recv_sem=o_r.at[step],
            device_id={"kc": to}, device_id_type=MESH)

    def came(step):
        source = lax.rem(me - step + devices, devices)
        pltpu.make_async_remote_copy(
            src_ref=occ.at[source, ia], dst_ref=occ.at[source, ia], send_sem=o_s.at[step],
            recv_sem=o_r.at[step], device_id={"kc": source}, device_id_type=MESH).wait_recv()

    def virtual(chip, way, own=False):
        place = virt.at[chip * 2 + core]
        send = {"right": right_s, "left": left_s, "pair": pair_s}[way]
        to = {"right": me + 2, "left": me - 2, "pair": z * 2 + 1 - core}[way]
        recv = pair_r if way == "pair" else v_r
        return pltpu.make_async_remote_copy(
            src_ref=virt_ref if own else place, dst_ref=place, send_sem=send.at[chip],
            recv_sem=recv.at[chip], device_id={"kc": to}, device_id_type=MESH)

    @pl.when(z < n - 1)
    def _():
        virtual(z, "right", True).start()

    @pl.when(z > 0)
    def _():
        virtual(z, "left", True).start()

    for step in range(1, devices):
        direct(step).start()
    virtual(z, "pair", True).start()
    virt[me] = virt_ref[...]
    for q in range(groups):
        occ[me, q] = occ_ref[q * share:(q + 1) * share, pl.ds(pl.multiple_of(me * cols, cols), cols)]

    spreads = []
    for step in range(1, devices):
        source = lax.rem(me - step + devices, devices)
        view = functools.partial(lambda source, i: occ.at[source, i], source)
        spreads.append(Spread(view, view(ia), step % 2, groups, g_s.at[step], g_r.at[step]))

    def hop(step):
        @pl.when(z - step >= 0)
        def _():
            virtual(z - step, "left").wait_recv()

            @pl.when(z < n - 1)
            def _():
                virtual(z - step, "right").start()

            virtual(z - step, "pair").start()

        @pl.when(z + step < n)
        def _():
            virtual(z + step, "left").wait_recv()

            @pl.when(z > 0)
            def _():
                virtual(z + step, "left").start()

            virtual(z + step, "pair").start()

    for step in range(1, devices):
        came(step)
        spreads[step - 1].start()
    hop(1)
    for spread in spreads:
        spread.relay()
    for step in range(2, n):
        hop(step)
    for spread in spreads:
        spread.finish()
    for chip in range(n):
        place = virt.at[chip * 2 + 1 - core]
        pltpu.make_async_remote_copy(
            src_ref=place, dst_ref=place, send_sem=pair_s.at[chip], recv_sem=pair_r.at[chip],
            device_id={"kc": z * 2 + 1 - core}, device_id_type=MESH).wait_recv()

    block = min(256, out_ref.shape[0])
    depth = devices * occ_ref.shape[0]

    def multiply(i, carry):
        at = pl.ds(pl.multiple_of(i * block, block), block)
        product = lax.dot_general(
            virt[:, :, at].reshape(depth, block), occ[...].reshape(depth, cols),
            (((0,), (0,)), ((), ())), preferred_element_type=jnp.float32)
        out_ref[at, :] = product.astype(jnp.bfloat16)
        return carry

    lax.fori_loop(0, out_ref.shape[0] // block, multiply, 0)

    for step in range(1, devices):
        direct(step).wait_send()
        spreads[step - 1].drain()
    for chip in range(n):
        virtual(chip, "pair").wait_send()

        @pl.when((chip <= z) & (z < n - 1))
        def _():
            virtual(chip, "right").wait_send()

        @pl.when((chip >= z) & (z > 0))
        def _():
            virtual(chip, "left").wait_send()


def transposed_integrals(occupied, virtual, devices, groups):
    share, cols = occupied.shape[0] // groups, occupied.shape[1] // devices
    n = devices // 2
    bf = jnp.bfloat16
    dma = pltpu.SemaphoreType.DMA
    vmem = pl.BlockSpec(memory_space=pltpu.VMEM)
    return pl.pallas_call(
        functools.partial(factors_kernel, devices, groups),
        out_shape=jax.ShapeDtypeStruct((virtual.shape[1], cols), bf),
        in_specs=[vmem, vmem],
        out_specs=vmem,
        scratch_shapes=[
            pltpu.VMEM((devices, groups, share, cols), bf),
            pltpu.VMEM((devices,) + virtual.shape, bf),
            dma((devices,)), dma((devices,)),
            dma((devices, groups // 2, 2)), dma((devices, groups // 2, 2)),
            dma((n,)), dma((n,)), dma((n,)), dma((n,)), dma((n,)),
        ],
        compiler_params=pltpu.CompilerParams(
            collective_id=1, has_side_effects=True, vmem_limit_bytes=40 * 2**20),
    )(occupied, virtual)


def reduce_kernel(
    n, groups, count, rows, a_ref, own_ref, o_ref,
    gathered, abuf, pair_out, pair_in, total, onward, from_left, from_right, kept, given,
    a_sem, pair_s, pair_r, right_s, right_r, left_s, left_r, kept_sem, given_s, given_r, g_s, g_r,
):
    me = lax.axis_index("kc")
    z, core = me // 2, me % 2
    width = own_ref.shape[2] // n
    half = width // 2
    partner = z * 2 + (1 - core)
    right, left = me + 2, me - 2

    def fetch(t, own):
        chunk = 2 * t + (core if own else 1 - core)
        start = pl.multiple_of(chunk * rows, rows)
        slot = 1 if own else 0
        return pltpu.make_async_copy(a_ref.at[pl.ds(start, rows)], abuf.at[slot], a_sem.at[slot])

    def pair(t):
        return pltpu.make_async_remote_copy(
            src_ref=pair_out.at[t], dst_ref=pair_in.at[t], send_sem=pair_s.at[t],
            recv_sem=pair_r.at[t], device_id={"kc": partner}, device_id_type=MESH)

    def go_right(t, d):
        return pltpu.make_async_remote_copy(
            src_ref=onward.at[t, d], dst_ref=from_left.at[t, d], send_sem=right_s.at[t, d],
            recv_sem=right_r.at[t, d], device_id={"kc": right}, device_id_type=MESH)

    def go_left(t, d):
        return pltpu.make_async_remote_copy(
            src_ref=onward.at[t, d], dst_ref=from_right.at[t, d], send_sem=left_s.at[t, d],
            recv_sem=left_r.at[t, d], device_id={"kc": left}, device_id_type=MESH)

    def keep(t):
        start = pl.multiple_of((2 * t + core) * rows, rows)
        return pltpu.make_async_copy(kept.at[t], o_ref.at[pl.ds(start, rows)], kept_sem.at[t])

    def give(t, whose):
        start = pl.multiple_of((2 * t + whose) * rows, rows)
        return pltpu.make_async_remote_copy(
            src_ref=given.at[t], dst_ref=o_ref.at[pl.ds(start, rows)], send_sem=given_s.at[t],
            recv_sem=given_r.at[t], device_id={"kc": partner}, device_id_type=MESH)

    ia = lax.axis_index("ia")
    k_half = own_ref.shape[0] // 2
    spreads = []
    for kind in range(2):
        ks = pl.ds(kind * k_half, k_half)
        view = functools.partial(lambda ks, i: gathered.at[ks, i], ks)
        spreads.append(Spread(view, own_ref.at[ks], kind, groups, g_s.at[kind], g_r.at[kind]))

    fetch(0, False).start()
    barrier = pltpu.get_barrier_semaphore()
    pl.semaphore_signal(barrier, inc=1, device_id={"kc": partner}, device_id_type=MESH)

    @pl.when(z > 0)
    def _():
        pl.semaphore_signal(barrier, inc=1, device_id={"kc": left}, device_id_type=MESH)

    @pl.when(z < n - 1)
    def _():
        pl.semaphore_signal(barrier, inc=1, device_id={"kc": right}, device_id_type=MESH)

    signal_all(barrier, "ia", groups)
    pl.semaphore_wait(barrier, groups + jnp.where(z > 0, 1, 0) + jnp.where(z < n - 1, 1, 0))
    for spread in spreads:
        spread.start()
    for k in range(own_ref.shape[0]):
        gathered[k, ia] = own_ref[k]
    for spread in spreads:
        spread.relay()
    for spread in spreads:
        spread.finish()

    def cycle():
        return gathered[...].reshape(-1, own_ref.shape[2])

    def columns(t, d):
        return total[t, :, d * width:(d + 1) * width]

    def step(t, carry):
        @pl.when(t < count)
        def _():
            fetch(t, False).wait()
            fetch(t, True).start()
            product = jnp.dot(abuf[0], cycle(), preferred_element_type=jnp.float32)
            pair_out[t] = product.astype(jnp.bfloat16)
            pair(t).start()
            fetch(t, True).wait()

            @pl.when(t + 1 < count)
            def _():
                fetch(t + 1, False).start()

            total[t] = jnp.dot(abuf[1], cycle(), preferred_element_type=jnp.float32)
            pair(t).wait_recv()
            total[t] += pair_in[t].astype(jnp.float32)

        tr = t - z

        @pl.when((tr >= 0) & (tr < count))
        def _():
            for d in reversed(range(1, n)):
                @pl.when((d > z) & (z == 0))
                def _():
                    onward[tr, d] = columns(tr, d).astype(jnp.bfloat16)
                    go_right(tr, d).start()

                @pl.when((d > z) & (z > 0))
                def _():
                    go_right(tr, d).wait_recv()
                    onward[tr, d] = (columns(tr, d) + from_left[tr, d].astype(jnp.float32)).astype(jnp.bfloat16)
                    go_right(tr, d).start()

        tl = t - (n - 1 - z)

        @pl.when((tl >= 0) & (tl < count))
        def _():
            for d in range(n - 1):
                @pl.when((d < z) & (z == n - 1))
                def _():
                    onward[tl, d] = columns(tl, d).astype(jnp.bfloat16)
                    go_left(tl, d).start()

                @pl.when((d < z) & (z < n - 1))
                def _():
                    go_left(tl, d).wait_recv()
                    onward[tl, d] = (columns(tl, d) + from_right[tl, d].astype(jnp.float32)).astype(jnp.bfloat16)
                    go_left(tl, d).start()

        tf = t - jnp.maximum(z, n - 1 - z)

        @pl.when((tf >= 0) & (tf < count))
        def _():
            for d in range(n):
                @pl.when(d == z)
                def _():
                    value = columns(tf, d)
                    if d > 0:
                        go_right(tf, d).wait_recv()
                        value += from_left[tf, d].astype(jnp.float32)
                    if d < n - 1:
                        go_left(tf, d).wait_recv()
                        value += from_right[tf, d].astype(jnp.float32)

                    @pl.when(core == 0)
                    def _():
                        kept[tf] = value[:, :half]
                        given[tf] = value[:, half:]

                    @pl.when(core == 1)
                    def _():
                        kept[tf] = value[:, half:]
                        given[tf] = value[:, :half]

            keep(tf).start()
            give(tf, core).start()

        return carry

    lax.fori_loop(0, count + n - 1, step, 0)

    def drain(t, carry):
        pair(t).wait_send()
        keep(t).wait()
        give(t, core).wait_send()
        give(t, 1 - core).wait_recv()
        for d in range(n):
            @pl.when(d > z)
            def _():
                go_right(t, d).wait_send()

            @pl.when(d < z)
            def _():
                go_left(t, d).wait_send()
        return carry

    lax.fori_loop(0, count, drain, 0)
    for spread in spreads:
        spread.drain()


def gemm_reduce_scatter(amplitudes, blocks, devices, groups):
    local_rows, depth = amplitudes.shape
    columns = blocks.shape[2]
    n = devices // 2
    rows = min(512, local_rows // 2)
    count = local_rows // (2 * rows)
    width = columns // n
    bf, f32 = jnp.bfloat16, jnp.float32
    dma = pltpu.SemaphoreType.DMA
    return pl.pallas_call(
        functools.partial(reduce_kernel, n, groups, count, rows),
        out_shape=jax.ShapeDtypeStruct((local_rows, width // 2), f32),
        in_specs=[pl.BlockSpec(memory_space=pl.ANY), pl.BlockSpec(memory_space=pltpu.VMEM)],
        out_specs=pl.BlockSpec(memory_space=pl.ANY),
        scratch_shapes=[
            pltpu.VMEM((blocks.shape[0], groups, blocks.shape[1], columns), bf),
            pltpu.VMEM((2, rows, depth), bf),
            pltpu.VMEM((count, rows, columns), bf),
            pltpu.VMEM((count, rows, columns), bf),
            pltpu.VMEM((count, rows, columns), f32),
            pltpu.VMEM((count, n, rows, width), bf),
            pltpu.VMEM((count, n, rows, width), bf),
            pltpu.VMEM((count, n, rows, width), bf),
            pltpu.VMEM((count, rows, width // 2), f32),
            pltpu.VMEM((count, rows, width // 2), f32),
            dma((2,)), dma((count,)), dma((count,)),
            dma((count, n)), dma((count, n)), dma((count, n)), dma((count, n)),
            dma((count,)), dma((count,)), dma((count,)),
            dma((2, groups // 2, 2)), dma((2, groups // 2, 2)),
        ],
        compiler_params=pltpu.CompilerParams(
            collective_id=0, has_side_effects=True, vmem_limit_bytes=60 * 2**20),
    )(amplitudes, blocks)


def per_device(amplitudes, occupied_factors, virtual_factors):
    devices, groups = lax.axis_size("kc"), lax.axis_size("ia")
    k_per_device = O // devices
    c_per_device = V // groups
    integrals = transposed_integrals(occupied_factors, virtual_factors, devices, groups)
    blocks = (
        integrals.reshape(c_per_device, BW, k_per_device, O)
        .transpose(2, 0, 3, 1)
        .reshape(k_per_device, c_per_device, O * BW)
    )
    return gemm_reduce_scatter(amplitudes, blocks, devices, groups)


def solution(mesh):
    placed = (P("ia", "kc"), P("kc", None), P("kc", "ia"))
    return jax.shard_map(
        per_device, mesh=mesh, in_specs=placed, out_specs=P("ia", "kc"), check_vma=False
    )
```

```python
import functools

import jax
import jax.numpy as jnp
from jax import lax
from jax.experimental import pallas as pl
from jax.experimental.pallas import tpu as pltpu
from jax.sharding import PartitionSpec as P

O = 64
V = 512
BW = 8
MESH = pl.DeviceIdType.MESH


class Spread:
    def __init__(self, view, own, kind, groups, send, recv):
        self.view, self.own, self.kind, self.send, self.recv = view, own, kind, send, recv
        self.a = 2
        self.b = groups // 2
        me = lax.axis_index("ia")
        self.p, self.q = me // self.b, me % self.b

    def at(self, r, s):
        return lax.rem(self.p + s + self.a, self.a) * self.b + lax.rem(self.q + r + self.b, self.b)

    def copy(self, source, r, s, target):
        return pltpu.make_async_remote_copy(
            src_ref=self.view(self.at(*source)) if source != (0, 0) else self.own,
            dst_ref=self.view(self.at(*source)), send_sem=self.send.at[r, s],
            recv_sem=self.recv.at[r, s], device_id={"ia": self.at(*target)}, device_id_type=MESH)

    def sends(self, direct):
        out = []
        for r in range(self.b):
            for s in range(self.a):
                if r and s and not direct:
                    out.append(self.copy((-r, 0), r, s, (0, s)) if self.kind == 0
                               else self.copy((0, -s), r, s, (r, 0)))
                elif (r or s) and not (r and s) and direct:
                    out.append(self.copy((0, 0), r, s, (r, s)))
        return out

    def arrived(self, r, s):
        pltpu.make_async_remote_copy(
            src_ref=self.view(self.at(-r, -s)), dst_ref=self.view(self.at(-r, -s)),
            send_sem=self.send.at[r, s], recv_sem=self.recv.at[r, s],
            device_id={"ia": self.at(r, s)}, device_id_type=MESH).wait_recv()

    def start(self):
        order = self.sends(True)
        for copy in order if self.kind else reversed(order):
            copy.start()

    def relay(self):
        if self.kind == 0:
            for r in range(1, self.b):
                self.arrived(r, 0)
        else:
            for s in range(1, self.a):
                self.arrived(0, s)
        for copy in self.sends(False):
            copy.start()

    def finish(self):
        for r in range(self.b):
            for s in range(self.a):
                first = (s == 0) if self.kind == 0 else (r == 0)
                if (r or s) and not first:
                    self.arrived(r, s)

    def drain(self):
        for copy in self.sends(True) + self.sends(False):
            copy.wait_send()


def signal_all(barrier, axis, size):
    me = lax.axis_index(axis)
    for step in range(1, size):
        pl.semaphore_signal(barrier, inc=1, device_id={axis: lax.rem(me + step, size)}, device_id_type=MESH)


def factors_kernel(
    devices, groups, occ_ref, virt_ref, out_ref, occ, virt,
    o_s, o_r, g_s, g_r, right_s, left_s, v_r, pair_s, pair_r,
):
    n = devices // 2
    me, ia = lax.axis_index("kc"), lax.axis_index("ia")
    z, core = me // 2, me % 2
    share = occ_ref.shape[0] // groups
    cols = occ_ref.shape[1] // devices

    barrier = pltpu.get_barrier_semaphore()
    signal_all(barrier, "kc", devices)
    signal_all(barrier, "ia", groups)
    pl.semaphore_wait(barrier, devices + groups - 2)

    def direct(step):
        to = lax.rem(me + step, devices)
        return pltpu.make_async_remote_copy(
            src_ref=occ_ref.at[pl.ds(pl.multiple_of(ia * share, share), share),
                               pl.ds(pl.multiple_of(to * cols, cols), cols)],
            dst_ref=occ.at[me, ia], send_sem=o_s.at[step], recv_sem=o_r.at[step],
            device_id={"kc": to}, device_id_type=MESH)

    def came(step):
        source = lax.rem(me - step + devices, devices)
        pltpu.make_async_remote_copy(
            src_ref=occ.at[source, ia], dst_ref=occ.at[source, ia], send_sem=o_s.at[step],
            recv_sem=o_r.at[step], device_id={"kc": source}, device_id_type=MESH).wait_recv()

    def virtual(chip, way, own=False):
        place = virt.at[chip * 2 + core]
        send = {"right": right_s, "left": left_s, "pair": pair_s}[way]
        to = {"right": me + 2, "left": me - 2, "pair": z * 2 + 1 - core}[way]
        recv = pair_r if way == "pair" else v_r
        return pltpu.make_async_remote_copy(
            src_ref=virt_ref if own else place, dst_ref=place, send_sem=send.at[chip],
            recv_sem=recv.at[chip], device_id={"kc": to}, device_id_type=MESH)

    @pl.when(z < n - 1)
    def _():
        virtual(z, "right", True).start()

    @pl.when(z > 0)
    def _():
        virtual(z, "left", True).start()

    for step in range(1, devices):
        direct(step).start()
    virtual(z, "pair", True).start()
    virt[me] = virt_ref[...]
    for q in range(groups):
        occ[me, q] = occ_ref[q * share:(q + 1) * share, pl.ds(pl.multiple_of(me * cols, cols), cols)]

    spreads = []
    for step in range(1, devices):
        source = lax.rem(me - step + devices, devices)
        view = functools.partial(lambda source, i: occ.at[source, i], source)
        spreads.append(Spread(view, view(ia), step % 2, groups, g_s.at[step], g_r.at[step]))

    def hop(step):
        @pl.when(z - step >= 0)
        def _():
            virtual(z - step, "left").wait_recv()

            @pl.when(z < n - 1)
            def _():
                virtual(z - step, "right").start()

            virtual(z - step, "pair").start()

        @pl.when(z + step < n)
        def _():
            virtual(z + step, "left").wait_recv()

            @pl.when(z > 0)
            def _():
                virtual(z + step, "left").start()

            virtual(z + step, "pair").start()

    for step in range(1, devices):
        came(step)
        spreads[step - 1].start()
    hop(1)
    for spread in spreads:
        spread.relay()
    for step in range(2, n):
        hop(step)
    for spread in spreads:
        spread.finish()
    for chip in range(n):
        place = virt.at[chip * 2 + 1 - core]
        pltpu.make_async_remote_copy(
            src_ref=place, dst_ref=place, send_sem=pair_s.at[chip], recv_sem=pair_r.at[chip],
            device_id={"kc": z * 2 + 1 - core}, device_id_type=MESH).wait_recv()

    block = min(256, out_ref.shape[0])
    depth = devices * occ_ref.shape[0]

    def multiply(i, carry):
        at = pl.ds(pl.multiple_of(i * block, block), block)
        product = lax.dot_general(
            virt[:, :, at].reshape(depth, block), occ[...].reshape(depth, cols),
            (((0,), (0,)), ((), ())), preferred_element_type=jnp.float32)
        out_ref[at, :] = product.astype(jnp.bfloat16)
        return carry

    lax.fori_loop(0, out_ref.shape[0] // block, multiply, 0)

    for step in range(1, devices):
        direct(step).wait_send()
        spreads[step - 1].drain()
    for chip in range(n):
        virtual(chip, "pair").wait_send()

        @pl.when((chip <= z) & (z < n - 1))
        def _():
            virtual(chip, "right").wait_send()

        @pl.when((chip >= z) & (z > 0))
        def _():
            virtual(chip, "left").wait_send()


def transposed_integrals(occupied, virtual, devices, groups):
    share, cols = occupied.shape[0] // groups, occupied.shape[1] // devices
    n = devices // 2
    bf = jnp.bfloat16
    dma = pltpu.SemaphoreType.DMA
    vmem = pl.BlockSpec(memory_space=pltpu.VMEM)
    return pl.pallas_call(
        functools.partial(factors_kernel, devices, groups),
        out_shape=jax.ShapeDtypeStruct((virtual.shape[1], cols), bf),
        in_specs=[vmem, vmem],
        out_specs=vmem,
        scratch_shapes=[
            pltpu.VMEM((devices, groups, share, cols), bf),
            pltpu.VMEM((devices,) + virtual.shape, bf),
            dma((devices,)), dma((devices,)),
            dma((devices, groups // 2, 2)), dma((devices, groups // 2, 2)),
            dma((n,)), dma((n,)), dma((n,)), dma((n,)), dma((n,)),
        ],
        compiler_params=pltpu.CompilerParams(
            collective_id=1, has_side_effects=True, vmem_limit_bytes=40 * 2**20),
    )(occupied, virtual)


def reduce_kernel(
    n, groups, count, rows, a_ref, own_ref, o_ref,
    gathered, abuf, pair_out, pair_in, total, onward, from_left, from_right, kept, given,
    a_sem, pair_s, pair_r, right_s, right_r, left_s, left_r, kept_sem, given_s, given_r, g_s, g_r,
):
    me = lax.axis_index("kc")
    z, core = me // 2, me % 2
    width = own_ref.shape[2] // n
    half = width // 2
    partner = z * 2 + (1 - core)
    right, left = me + 2, me - 2

    def fetch(t, own):
        chunk = 2 * t + (core if own else 1 - core)
        start = pl.multiple_of(chunk * rows, rows)
        slot = 1 if own else 0
        return pltpu.make_async_copy(a_ref.at[pl.ds(start, rows)], abuf.at[slot], a_sem.at[slot])

    def pair(t):
        return pltpu.make_async_remote_copy(
            src_ref=pair_out.at[t], dst_ref=pair_in.at[t], send_sem=pair_s.at[t],
            recv_sem=pair_r.at[t], device_id={"kc": partner}, device_id_type=MESH)

    def go_right(t, d):
        return pltpu.make_async_remote_copy(
            src_ref=onward.at[t, d], dst_ref=from_left.at[t, d], send_sem=right_s.at[t, d],
            recv_sem=right_r.at[t, d], device_id={"kc": right}, device_id_type=MESH)

    def go_left(t, d):
        return pltpu.make_async_remote_copy(
            src_ref=onward.at[t, d], dst_ref=from_right.at[t, d], send_sem=left_s.at[t, d],
            recv_sem=left_r.at[t, d], device_id={"kc": left}, device_id_type=MESH)

    def keep(t):
        start = pl.multiple_of((2 * t + core) * rows, rows)
        return pltpu.make_async_copy(kept.at[t], o_ref.at[:, pl.ds(start, rows)], kept_sem.at[t])

    def give(t, whose):
        start = pl.multiple_of((2 * t + whose) * rows, rows)
        return pltpu.make_async_remote_copy(
            src_ref=given.at[t], dst_ref=o_ref.at[:, pl.ds(start, rows)], send_sem=given_s.at[t],
            recv_sem=given_r.at[t], device_id={"kc": partner}, device_id_type=MESH)

    ia = lax.axis_index("ia")
    k_half = own_ref.shape[0] // 2
    spreads = []
    for kind in range(2):
        ks = pl.ds(kind * k_half, k_half)
        view = functools.partial(lambda ks, i: gathered.at[ks, i], ks)
        spreads.append(Spread(view, own_ref.at[ks], kind, groups, g_s.at[kind], g_r.at[kind]))

    fetch(0, False).start()
    barrier = pltpu.get_barrier_semaphore()
    pl.semaphore_signal(barrier, inc=1, device_id={"kc": partner}, device_id_type=MESH)

    @pl.when(z > 0)
    def _():
        pl.semaphore_signal(barrier, inc=1, device_id={"kc": left}, device_id_type=MESH)

    @pl.when(z < n - 1)
    def _():
        pl.semaphore_signal(barrier, inc=1, device_id={"kc": right}, device_id_type=MESH)

    signal_all(barrier, "ia", groups)
    pl.semaphore_wait(barrier, groups + jnp.where(z > 0, 1, 0) + jnp.where(z < n - 1, 1, 0))
    for spread in spreads:
        spread.start()
    for k in range(own_ref.shape[0]):
        gathered[k, ia] = own_ref[k]
    for spread in spreads:
        spread.relay()
    for spread in spreads:
        spread.finish()

    def cycle():
        return gathered[...].reshape(-1, own_ref.shape[2])

    def columns(t, d):
        return total[t, :, d * width:(d + 1) * width]

    def step(t, carry):
        @pl.when(t < count)
        def _():
            fetch(t, False).wait()
            fetch(t, True).start()
            product = jnp.dot(abuf[0], cycle(), preferred_element_type=jnp.float32)
            pair_out[t] = product.astype(jnp.bfloat16)
            pair(t).start()
            fetch(t, True).wait()

            @pl.when(t + 1 < count)
            def _():
                fetch(t + 1, False).start()

            total[t] = jnp.dot(abuf[1], cycle(), preferred_element_type=jnp.float32)
            pair(t).wait_recv()
            total[t] += pair_in[t].astype(jnp.float32)

        tr = t - z

        @pl.when((tr >= 0) & (tr < count))
        def _():
            for d in reversed(range(1, n)):
                @pl.when((d > z) & (z == 0))
                def _():
                    onward[tr, d] = columns(tr, d).astype(jnp.bfloat16)
                    go_right(tr, d).start()

                @pl.when((d > z) & (z > 0))
                def _():
                    go_right(tr, d).wait_recv()
                    onward[tr, d] = (columns(tr, d) + from_left[tr, d].astype(jnp.float32)).astype(jnp.bfloat16)
                    go_right(tr, d).start()

        tl = t - (n - 1 - z)

        @pl.when((tl >= 0) & (tl < count))
        def _():
            for d in range(n - 1):
                @pl.when((d < z) & (z == n - 1))
                def _():
                    onward[tl, d] = columns(tl, d).astype(jnp.bfloat16)
                    go_left(tl, d).start()

                @pl.when((d < z) & (z < n - 1))
                def _():
                    go_left(tl, d).wait_recv()
                    onward[tl, d] = (columns(tl, d) + from_right[tl, d].astype(jnp.float32)).astype(jnp.bfloat16)
                    go_left(tl, d).start()

        tf = t - jnp.maximum(z, n - 1 - z)

        @pl.when((tf >= 0) & (tf < count))
        def _():
            for d in range(n):
                @pl.when(d == z)
                def _():
                    value = columns(tf, d)
                    if d > 0:
                        go_right(tf, d).wait_recv()
                        value += from_left[tf, d].astype(jnp.float32)
                    if d < n - 1:
                        go_left(tf, d).wait_recv()
                        value += from_right[tf, d].astype(jnp.float32)

                    value = value.T

                    @pl.when(core == 0)
                    def _():
                        kept[tf] = value[:half]
                        given[tf] = value[half:]

                    @pl.when(core == 1)
                    def _():
                        kept[tf] = value[half:]
                        given[tf] = value[:half]

            keep(tf).start()
            give(tf, core).start()

        return carry

    lax.fori_loop(0, count + n - 1, step, 0)

    def drain(t, carry):
        pair(t).wait_send()
        keep(t).wait()
        give(t, core).wait_send()
        give(t, 1 - core).wait_recv()
        for d in range(n):
            @pl.when(d > z)
            def _():
                go_right(t, d).wait_send()

            @pl.when(d < z)
            def _():
                go_left(t, d).wait_send()
        return carry

    lax.fori_loop(0, count, drain, 0)
    for spread in spreads:
        spread.drain()


def gemm_reduce_scatter(amplitudes, blocks, devices, groups):
    local_rows, depth = amplitudes.shape
    columns = blocks.shape[2]
    n = devices // 2
    rows = min(256, local_rows // 2)
    count = local_rows // (2 * rows)
    width = columns // n
    bf, f32 = jnp.bfloat16, jnp.float32
    dma = pltpu.SemaphoreType.DMA
    return pl.pallas_call(
        functools.partial(reduce_kernel, n, groups, count, rows),
        out_shape=jax.ShapeDtypeStruct((width // 2, local_rows), f32),
        in_specs=[pl.BlockSpec(memory_space=pl.ANY), pl.BlockSpec(memory_space=pltpu.VMEM)],
        out_specs=pl.BlockSpec(memory_space=pl.ANY),
        scratch_shapes=[
            pltpu.VMEM((blocks.shape[0], groups, blocks.shape[1], columns), bf),
            pltpu.VMEM((2, rows, depth), bf),
            pltpu.VMEM((count, rows, columns), bf),
            pltpu.VMEM((count, rows, columns), bf),
            pltpu.VMEM((count, rows, columns), f32),
            pltpu.VMEM((count, n, rows, width), bf),
            pltpu.VMEM((count, n, rows, width), bf),
            pltpu.VMEM((count, n, rows, width), bf),
            pltpu.VMEM((count, width // 2, rows), f32),
            pltpu.VMEM((count, width // 2, rows), f32),
            dma((2,)), dma((count,)), dma((count,)),
            dma((count, n)), dma((count, n)), dma((count, n)), dma((count, n)),
            dma((count,)), dma((count,)), dma((count,)),
            dma((2, groups // 2, 2)), dma((2, groups // 2, 2)),
        ],
        compiler_params=pltpu.CompilerParams(
            collective_id=0, has_side_effects=True, vmem_limit_bytes=60 * 2**20),
    )(amplitudes, blocks).T


def per_device(amplitudes, occupied_factors, virtual_factors):
    devices, groups = lax.axis_size("kc"), lax.axis_size("ia")
    k_per_device = O // devices
    c_per_device = V // groups
    integrals = transposed_integrals(occupied_factors, virtual_factors, devices, groups)
    blocks = (
        integrals.reshape(c_per_device, BW, k_per_device, O)
        .transpose(2, 0, 3, 1)
        .reshape(k_per_device, c_per_device, O * BW)
    )
    return gemm_reduce_scatter(amplitudes, blocks, devices, groups)


def solution(mesh):
    placed = (P("ia", "kc"), P("kc", None), P("kc", "ia"))
    return jax.shard_map(
        per_device, mesh=mesh, in_specs=placed, out_specs=P("ia", "kc"), check_vma=False
    )
```

```python
import functools

import jax
import jax.numpy as jnp
from jax import lax
from jax.experimental import pallas as pl
from jax.experimental.pallas import tpu as pltpu
from jax.sharding import PartitionSpec as P

O = 64
V = 512
BW = 8
MESH = pl.DeviceIdType.MESH


class Spread:
    def __init__(self, view, own, kind, groups, send, recv):
        self.view, self.own, self.kind, self.send, self.recv = view, own, kind, send, recv
        self.a = 2
        self.b = groups // 2
        me = lax.axis_index("ia")
        self.p, self.q = me // self.b, me % self.b

    def at(self, r, s):
        return lax.rem(self.p + s + self.a, self.a) * self.b + lax.rem(self.q + r + self.b, self.b)

    def copy(self, source, r, s, target):
        return pltpu.make_async_remote_copy(
            src_ref=self.view(self.at(*source)) if source != (0, 0) else self.own,
            dst_ref=self.view(self.at(*source)), send_sem=self.send.at[r, s],
            recv_sem=self.recv.at[r, s], device_id={"ia": self.at(*target)}, device_id_type=MESH)

    def sends(self, direct):
        out = []
        for r in range(self.b):
            for s in range(self.a):
                if r and s and not direct:
                    out.append(self.copy((-r, 0), r, s, (0, s)) if self.kind == 0
                               else self.copy((0, -s), r, s, (r, 0)))
                elif (r or s) and not (r and s) and direct:
                    out.append(self.copy((0, 0), r, s, (r, s)))
        return out

    def arrived(self, r, s):
        pltpu.make_async_remote_copy(
            src_ref=self.view(self.at(-r, -s)), dst_ref=self.view(self.at(-r, -s)),
            send_sem=self.send.at[r, s], recv_sem=self.recv.at[r, s],
            device_id={"ia": self.at(r, s)}, device_id_type=MESH).wait_recv()

    def start(self):
        order = self.sends(True)
        for copy in order if self.kind else reversed(order):
            copy.start()

    def relay(self):
        if self.kind == 0:
            for r in range(1, self.b):
                self.arrived(r, 0)
        else:
            for s in range(1, self.a):
                self.arrived(0, s)
        for copy in self.sends(False):
            copy.start()

    def finish(self):
        for r in range(self.b):
            for s in range(self.a):
                first = (s == 0) if self.kind == 0 else (r == 0)
                if (r or s) and not first:
                    self.arrived(r, s)

    def drain(self):
        for copy in self.sends(True) + self.sends(False):
            copy.wait_send()


def signal_all(barrier, axis, size):
    me = lax.axis_index(axis)
    for step in range(1, size):
        pl.semaphore_signal(barrier, inc=1, device_id={axis: lax.rem(me + step, size)}, device_id_type=MESH)


def factors_kernel(
    devices, groups, occ_ref, virt_ref, out_ref, occ, virt, total,
    o_s, o_r, g_s, g_r, right_s, left_s, v_r, pair_s, pair_r, mine_s,
):
    n = devices // 2
    me, ia = lax.axis_index("kc"), lax.axis_index("ia")
    z, core = me // 2, me % 2
    share = occ_ref.shape[0] // groups
    cols = occ_ref.shape[1] // devices

    barrier = pltpu.get_barrier_semaphore()
    signal_all(barrier, "kc", devices)
    signal_all(barrier, "ia", groups)
    pl.semaphore_wait(barrier, devices + groups - 2)

    def direct(step):
        to = lax.rem(me + step, devices)
        return pltpu.make_async_remote_copy(
            src_ref=occ_ref.at[pl.ds(pl.multiple_of(ia * share, share), share),
                               pl.ds(pl.multiple_of(to * cols, cols), cols)],
            dst_ref=occ.at[me, ia], send_sem=o_s.at[step], recv_sem=o_r.at[step],
            device_id={"kc": to}, device_id_type=MESH)

    def came(step):
        source = lax.rem(me - step + devices, devices)
        pltpu.make_async_remote_copy(
            src_ref=occ.at[source, ia], dst_ref=occ.at[source, ia], send_sem=o_s.at[step],
            recv_sem=o_r.at[step], device_id={"kc": source}, device_id_type=MESH).wait_recv()

    def virtual(chip, way, own=False):
        place = virt.at[chip * 2 + core]
        send = {"right": right_s, "left": left_s, "pair": pair_s}[way]
        to = {"right": me + 2, "left": me - 2, "pair": z * 2 + 1 - core}[way]
        recv = pair_r if way == "pair" else v_r
        return pltpu.make_async_remote_copy(
            src_ref=virt_ref if own else place, dst_ref=place, send_sem=send.at[chip],
            recv_sem=recv.at[chip], device_id={"kc": to}, device_id_type=MESH)

    @pl.when(z < n - 1)
    def _():
        virtual(z, "right", True).start()

    @pl.when(z > 0)
    def _():
        virtual(z, "left", True).start()

    for step in range(1, devices):
        direct(step).start()
    virtual(z, "pair", True).start()
    mine = [pltpu.make_async_copy(virt_ref, virt.at[me], mine_s.at[groups])]
    for q in range(groups):
        mine.append(pltpu.make_async_copy(
            occ_ref.at[pl.ds(q * share, share), pl.ds(pl.multiple_of(me * cols, cols), cols)],
            occ.at[me, q], mine_s.at[q]))
    for copy in mine:
        copy.start()
    total[...] = jnp.zeros_like(total)

    spreads = []
    for step in range(1, devices):
        source = lax.rem(me - step + devices, devices)
        view = functools.partial(lambda source, i: occ.at[source, i], source)
        spreads.append(Spread(view, view(ia), step % 2, groups, g_s.at[step], g_r.at[step]))

    def hop(step):
        @pl.when(z - step >= 0)
        def _():
            virtual(z - step, "left").wait_recv()

            @pl.when(z < n - 1)
            def _():
                virtual(z - step, "right").start()

            virtual(z - step, "pair").start()

        @pl.when(z + step < n)
        def _():
            virtual(z + step, "left").wait_recv()

            @pl.when(z > 0)
            def _():
                virtual(z + step, "left").start()

            virtual(z + step, "pair").start()

    for step in range(1, devices):
        came(step)
        spreads[step - 1].start()
    hop(1)
    for spread in spreads:
        spread.relay()
    for step in range(2, n - 1):
        hop(step)
    for spread in spreads:
        spread.finish()
    for copy in mine:
        copy.wait()
    block = min(256, out_ref.shape[0])
    depth = 2 * occ_ref.shape[0]

    def add_chip(chip):
        place = virt.at[chip * 2 + 1 - core]
        pltpu.make_async_remote_copy(
            src_ref=place, dst_ref=place, send_sem=pair_s.at[chip], recv_sem=pair_r.at[chip],
            device_id={"kc": z * 2 + 1 - core}, device_id_type=MESH).wait_recv()
        rows = slice(2 * chip, 2 * chip + 2)

        def multiply(i, carry):
            at = pl.ds(pl.multiple_of(i * block, block), block)
            total[at, :] += lax.dot_general(
                virt[rows, :, at].reshape(depth, block), occ[rows].reshape(depth, cols),
                (((0,), (0,)), ((), ())), preferred_element_type=jnp.float32)
            return carry

        lax.fori_loop(0, out_ref.shape[0] // block, multiply, 0)

    for chip in range(n):
        @pl.when((chip - z < n - 1) & (z - chip < n - 1))
        def _():
            add_chip(chip)

    if n > 2:
        hop(n - 1)
    for chip in (0, n - 1):
        @pl.when((chip - z == n - 1) | (z - chip == n - 1))
        def _():
            add_chip(chip)

    out_ref[...] = total[...].astype(jnp.bfloat16)

    for step in range(1, devices):
        direct(step).wait_send()
        spreads[step - 1].drain()
    for chip in range(n):
        virtual(chip, "pair").wait_send()

        @pl.when((chip <= z) & (z < n - 1))
        def _():
            virtual(chip, "right").wait_send()

        @pl.when((chip >= z) & (z > 0))
        def _():
            virtual(chip, "left").wait_send()


def transposed_integrals(occupied, virtual, devices, groups):
    share, cols = occupied.shape[0] // groups, occupied.shape[1] // devices
    n = devices // 2
    bf = jnp.bfloat16
    dma = pltpu.SemaphoreType.DMA
    vmem = pl.BlockSpec(memory_space=pltpu.VMEM)
    return pl.pallas_call(
        functools.partial(factors_kernel, devices, groups),
        out_shape=jax.ShapeDtypeStruct((virtual.shape[1], cols), bf),
        in_specs=[pl.BlockSpec(memory_space=pl.ANY)] * 2,
        out_specs=vmem,
        scratch_shapes=[
            pltpu.VMEM((devices, groups, share, cols), bf),
            pltpu.VMEM((devices,) + virtual.shape, bf),
            pltpu.VMEM((virtual.shape[1], cols), jnp.float32),
            dma((devices,)), dma((devices,)),
            dma((devices, groups // 2, 2)), dma((devices, groups // 2, 2)),
            dma((n,)), dma((n,)), dma((n,)), dma((n,)), dma((n,)), dma((groups + 1,)),
        ],
        compiler_params=pltpu.CompilerParams(
            collective_id=1, has_side_effects=True, vmem_limit_bytes=60 * 2**20),
    )(occupied, virtual)


def reduce_kernel(
    n, groups, count, rows, a_ref, own_ref, o_ref,
    gathered, abuf, pair_out, pair_in, total, onward, from_left, from_right, kept, given,
    a_sem, pair_s, pair_r, right_s, right_r, left_s, left_r, kept_sem, given_s, given_r, g_s, g_r,
):
    me = lax.axis_index("kc")
    z, core = me // 2, me % 2
    width = own_ref.shape[2] // n
    half = width // 2
    partner = z * 2 + (1 - core)
    right, left = me + 2, me - 2

    def fetch(t, own):
        chunk = 2 * t + (core if own else 1 - core)
        start = pl.multiple_of(chunk * rows, rows)
        slot = 1 if own else 0
        return pltpu.make_async_copy(a_ref.at[pl.ds(start, rows)], abuf.at[slot], a_sem.at[slot])

    def pair(t):
        return pltpu.make_async_remote_copy(
            src_ref=pair_out.at[t], dst_ref=pair_in.at[t], send_sem=pair_s.at[t],
            recv_sem=pair_r.at[t], device_id={"kc": partner}, device_id_type=MESH)

    def go_right(t, d):
        return pltpu.make_async_remote_copy(
            src_ref=onward.at[t, d], dst_ref=from_left.at[t, d], send_sem=right_s.at[t, d],
            recv_sem=right_r.at[t, d], device_id={"kc": right}, device_id_type=MESH)

    def go_left(t, d):
        return pltpu.make_async_remote_copy(
            src_ref=onward.at[t, d], dst_ref=from_right.at[t, d], send_sem=left_s.at[t, d],
            recv_sem=left_r.at[t, d], device_id={"kc": left}, device_id_type=MESH)

    def keep(t):
        start = pl.multiple_of((2 * t + core) * rows, rows)
        return pltpu.make_async_copy(kept.at[t], o_ref.at[:, pl.ds(start, rows)], kept_sem.at[t])

    def give(t, whose):
        start = pl.multiple_of((2 * t + whose) * rows, rows)
        return pltpu.make_async_remote_copy(
            src_ref=given.at[t], dst_ref=o_ref.at[:, pl.ds(start, rows)], send_sem=given_s.at[t],
            recv_sem=given_r.at[t], device_id={"kc": partner}, device_id_type=MESH)

    ia = lax.axis_index("ia")
    k_half = own_ref.shape[0] // 2
    spreads = []
    for kind in range(2):
        ks = pl.ds(kind * k_half, k_half)
        view = functools.partial(lambda ks, i: gathered.at[ks, i], ks)
        spreads.append(Spread(view, own_ref.at[ks], kind, groups, g_s.at[kind], g_r.at[kind]))

    fetch(0, False).start()
    barrier = pltpu.get_barrier_semaphore()
    pl.semaphore_signal(barrier, inc=1, device_id={"kc": partner}, device_id_type=MESH)

    @pl.when(z > 0)
    def _():
        pl.semaphore_signal(barrier, inc=1, device_id={"kc": left}, device_id_type=MESH)

    @pl.when(z < n - 1)
    def _():
        pl.semaphore_signal(barrier, inc=1, device_id={"kc": right}, device_id_type=MESH)

    signal_all(barrier, "ia", groups)
    pl.semaphore_wait(barrier, groups + jnp.where(z > 0, 1, 0) + jnp.where(z < n - 1, 1, 0))
    for spread in spreads:
        spread.start()
    for k in range(own_ref.shape[0]):
        gathered[k, ia] = own_ref[k]
    for spread in spreads:
        spread.relay()
    for spread in spreads:
        spread.finish()

    def cycle():
        return gathered[...].reshape(-1, own_ref.shape[2])

    def columns(t, d):
        return total[t, :, d * width:(d + 1) * width]

    def step(t, carry):
        @pl.when(t < count)
        def _():
            fetch(t, False).wait()
            fetch(t, True).start()
            product = jnp.dot(abuf[0], cycle(), preferred_element_type=jnp.float32)
            pair_out[t] = product.astype(jnp.bfloat16)
            pair(t).start()
            fetch(t, True).wait()

            @pl.when(t + 1 < count)
            def _():
                fetch(t + 1, False).start()

            total[t] = jnp.dot(abuf[1], cycle(), preferred_element_type=jnp.float32)
            pair(t).wait_recv()
            total[t] += pair_in[t].astype(jnp.float32)

        tr = t - z

        @pl.when((tr >= 0) & (tr < count))
        def _():
            for d in reversed(range(1, n)):
                @pl.when((d > z) & (z == 0))
                def _():
                    onward[tr, d] = columns(tr, d).astype(jnp.bfloat16)
                    go_right(tr, d).start()

                @pl.when((d > z) & (z > 0))
                def _():
                    go_right(tr, d).wait_recv()
                    onward[tr, d] = (columns(tr, d) + from_left[tr, d].astype(jnp.float32)).astype(jnp.bfloat16)
                    go_right(tr, d).start()

        tl = t - (n - 1 - z)

        @pl.when((tl >= 0) & (tl < count))
        def _():
            for d in range(n - 1):
                @pl.when((d < z) & (z == n - 1))
                def _():
                    onward[tl, d] = columns(tl, d).astype(jnp.bfloat16)
                    go_left(tl, d).start()

                @pl.when((d < z) & (z < n - 1))
                def _():
                    go_left(tl, d).wait_recv()
                    onward[tl, d] = (columns(tl, d) + from_right[tl, d].astype(jnp.float32)).astype(jnp.bfloat16)
                    go_left(tl, d).start()

        tf = t - jnp.maximum(z, n - 1 - z)

        @pl.when((tf >= 0) & (tf < count))
        def _():
            for d in range(n):
                @pl.when(d == z)
                def _():
                    value = columns(tf, d)
                    if d > 0:
                        go_right(tf, d).wait_recv()
                        value += from_left[tf, d].astype(jnp.float32)
                    if d < n - 1:
                        go_left(tf, d).wait_recv()
                        value += from_right[tf, d].astype(jnp.float32)

                    value = value.T

                    @pl.when(core == 0)
                    def _():
                        kept[tf] = value[:half]
                        given[tf] = value[half:]

                    @pl.when(core == 1)
                    def _():
                        kept[tf] = value[half:]
                        given[tf] = value[:half]

            keep(tf).start()
            give(tf, core).start()

        return carry

    lax.fori_loop(0, count + n - 1, step, 0)

    def drain(t, carry):
        pair(t).wait_send()
        keep(t).wait()
        give(t, core).wait_send()
        give(t, 1 - core).wait_recv()
        for d in range(n):
            @pl.when(d > z)
            def _():
                go_right(t, d).wait_send()

            @pl.when(d < z)
            def _():
                go_left(t, d).wait_send()
        return carry

    lax.fori_loop(0, count, drain, 0)
    for spread in spreads:
        spread.drain()


def gemm_reduce_scatter(amplitudes, blocks, devices, groups):
    local_rows, depth = amplitudes.shape
    columns = blocks.shape[2]
    n = devices // 2
    rows = min(256, local_rows // 2)
    count = local_rows // (2 * rows)
    width = columns // n
    bf, f32 = jnp.bfloat16, jnp.float32
    dma = pltpu.SemaphoreType.DMA
    return pl.pallas_call(
        functools.partial(reduce_kernel, n, groups, count, rows),
        out_shape=jax.ShapeDtypeStruct((width // 2, local_rows), f32),
        in_specs=[pl.BlockSpec(memory_space=pl.ANY), pl.BlockSpec(memory_space=pltpu.VMEM)],
        out_specs=pl.BlockSpec(memory_space=pl.ANY),
        scratch_shapes=[
            pltpu.VMEM((blocks.shape[0], groups, blocks.shape[1], columns), bf),
            pltpu.VMEM((2, rows, depth), bf),
            pltpu.VMEM((count, rows, columns), bf),
            pltpu.VMEM((count, rows, columns), bf),
            pltpu.VMEM((count, rows, columns), f32),
            pltpu.VMEM((count, n, rows, width), bf),
            pltpu.VMEM((count, n, rows, width), bf),
            pltpu.VMEM((count, n, rows, width), bf),
            pltpu.VMEM((count, width // 2, rows), f32),
            pltpu.VMEM((count, width // 2, rows), f32),
            dma((2,)), dma((count,)), dma((count,)),
            dma((count, n)), dma((count, n)), dma((count, n)), dma((count, n)),
            dma((count,)), dma((count,)), dma((count,)),
            dma((2, groups // 2, 2)), dma((2, groups // 2, 2)),
        ],
        compiler_params=pltpu.CompilerParams(
            collective_id=0, has_side_effects=True, vmem_limit_bytes=60 * 2**20),
    )(amplitudes, blocks).T


def per_device(amplitudes, occupied_factors, virtual_factors):
    devices, groups = lax.axis_size("kc"), lax.axis_size("ia")
    k_per_device = O // devices
    c_per_device = V // groups
    integrals = transposed_integrals(occupied_factors, virtual_factors, devices, groups)
    blocks = (
        integrals.reshape(c_per_device, BW, k_per_device, O)
        .transpose(2, 0, 3, 1)
        .reshape(k_per_device, c_per_device, O * BW)
    )
    return gemm_reduce_scatter(amplitudes, blocks, devices, groups)


def solution(mesh):
    placed = (P("ia", "kc"), P("kc", None), P("kc", "ia"))
    return jax.shard_map(
        per_device, mesh=mesh, in_specs=placed, out_specs=P("ia", "kc"), check_vma=False
    )
```
